32 devices in a mesh: groups: 2 (over x), wide: 16 (over z, y, core).
Axes of the slice: x: 2, y: 2, z: 4, core: 2. Of those that a mesh axis runs over, the one named last changes fastest.
Arguments:
- queries: bfloat16 [4096, 512], P(('groups', 'wide')), parts along dimension 0, may hold values from -200 to 200, as said below
- tree_kv: bfloat16 [2, 4096, 128], P(None, ('groups', 'wide')), parts along dimension 1, may hold values from -7 to 7, as said below
- kv_cache: bfloat16 [2, 512, 32, 128], P(None, ('groups', 'wide')), parts along dimension 1, may hold values from -6 to 6, as said below
- block_table: int32 [128, 4], P(('groups', 'wide')), parts along dimension 0, may hold values from 0 to 15, as said below
- cache_lengths: int32 [32, 4], P(('groups', 'wide')), parts along dimension 0, may hold values from 1 to 128, as said below
- parents: int32 [128, 32], P(('groups', 'wide')), parts along dimension 0, may hold values from -1 to 30, as said below
- w_out: bfloat16 [8192, 2048], P('wide'), may hold values from -0.375 to 0.375, as said below
- w_gate: bfloat16 [16, 2048, 768], P('wide'), may hold values from -0.125 to 0.125
- w_up: bfloat16 [16, 2048, 768], P('wide'), may hold values from -0.125 to 0.125
- w_down: bfloat16 [16, 768, 2048], P('wide'), may hold values from -0.4375 to 0.4375
- expert_ids: int32 [512, 8], P(('groups', 'wide')), parts along dimension 0, may hold values from 0 to 15, as said below
- gate_weights: float32 [512, 8], P(('groups', 'wide')), parts along dimension 0, may hold values from 0.05 to 0.5
Outputs:
- mixed: bfloat16 [512, 2048], P(('groups', 'wide')), parts along dimension 0
The draws below stay inside these ranges and needn't reach their ends.
There are 2 independent parts, one for each index of `groups`. The reference program is written for one: setup_inputs(seed, part) draws one part's arguments, and reference() takes and returns one part's arrays. A program takes and returns all parts, laid end to end along the dimension named above; an argument that names none is the same for every part. Nothing has to cross between parts.
Inputs may be any that keep to these rules, and one draw needn't show every extreme that they name: `queries`: its hidden draw may carry large entries. `tree_kv`: blocks of one group whose slices use the same key head are equal. `kv_cache`: pools of one group whose slices use the same key head are equal. `block_table`: each device's rows list every page of its pool once; blocks t * 2 + g are equal for all t. `cache_lengths`: rows t * 2 + g are equal for all t; every row holds one length 128 and one length 1. `parents`: node i of a tree has a parent before it; node 0 is the root with parent -1; blocks t * 2 + g are equal for all t. `w_out`: blocks of one head slice are equal. `expert_ids`: each row lists 8 different experts. Within the rows of one device no expert is listed by more than 10 rows; in every draw one expert is listed by exactly 10 rows of every device.
All inputs are finite; a program needn't handle non-finite values.
Results may differ from the reference program's by a relative error of at most 0.0083.
Values may be sent and summed in bfloat16 or wider, within the bound.
A program may use at most 64 MiB of HBM per device.

```python
import math
import jax
import jax.numpy as jnp
from jax import lax

D_MODEL = 2048
KV_HEADS = 4
HEAD_DIM = 128
FF_EXP = 768
TOP_K = 8
EXPERTS = 16
ATT_TP = 8
QH_DEV = 4
HEAD_SLICE = 512
GROUPS = 2
TREE_ROWS = 32
GROUP_SEQS = 4
PAGE_LEN = 32
PAGES_SEQ = 4
CACHE_MAX = 128
POOL_DEV = 16
ROWS_G = 128
ROWS_DEV = 16
TOKENS = 256
MEAN_LOAD = 8
MOST_ROWS = 10
N_WIDE = 16


def device_heads():
    devices = jnp.arange(ATT_TP * GROUPS, dtype=jnp.int32)
    return (devices // GROUPS // (ATT_TP // KV_HEADS), devices % GROUPS)


def by_group(base):
    return jnp.tile(base, (ATT_TP,) + (1,) * (base.ndim - 1))


def node_keys(key):
    source = jax.random.fold_in(key, 7001)
    return jnp.clip(jax.random.normal(source, (KV_HEADS, GROUPS, ROWS_G, HEAD_DIM), jnp.float32), -6.0, 6.0)


def draw_tree_kv(key, part):
    key_rows = node_keys(key)
    value_rows = jnp.clip(jax.random.normal(jax.random.fold_in(key, 7002), (KV_HEADS, GROUPS, ROWS_G, HEAD_DIM), jnp.float32), -6.0, 6.0)
    head_ids, group_ids = device_heads()
    stacked = jnp.stack([key_rows[head_ids, group_ids], value_rows[head_ids, group_ids]])
    return stacked.reshape(2, ATT_TP * GROUPS * ROWS_G, HEAD_DIM).astype(jnp.bfloat16)


def draw_queries(key, part):
    device_count = ATT_TP * GROUPS
    drawn = jnp.clip(jax.random.normal(jax.random.fold_in(key, 7003), (device_count, GROUP_SEQS, TREE_ROWS, HEAD_SLICE), jnp.float32), -6.0, 6.0)
    return drawn.reshape(device_count * ROWS_G, HEAD_SLICE).astype(jnp.bfloat16)


def draw_kv_cache(key, part):
    base = jnp.clip(jax.random.normal(jax.random.fold_in(key, 7009), (2, KV_HEADS, GROUPS, POOL_DEV, PAGE_LEN, HEAD_DIM), jnp.float32), -6.0, 6.0)
    head_ids, group_ids = device_heads()
    spread = base[:, head_ids, group_ids]
    return spread.reshape(2, ATT_TP * GROUPS * POOL_DEV, PAGE_LEN, HEAD_DIM).astype(jnp.bfloat16)


def draw_block_table(key, part):
    group_keys = jax.random.split(jax.random.fold_in(key, 7005), GROUPS)
    orders = jax.vmap(lambda single: jax.random.permutation(single, POOL_DEV))(group_keys)
    tables = by_group(orders.reshape(GROUPS, GROUP_SEQS, PAGES_SEQ))
    return tables.reshape(ATT_TP * GROUPS * GROUP_SEQS, PAGES_SEQ).astype(jnp.int32)


def draw_cache_lengths(key, part):
    lengths = jax.random.randint(jax.random.fold_in(key, 7010), (GROUPS, GROUP_SEQS), 1, CACHE_MAX + 1, dtype=jnp.int32)
    longest = jax.random.randint(jax.random.fold_in(key, 7011), (GROUPS, 1), 0, GROUP_SEQS, dtype=jnp.int32)
    shortest = (longest + 1) % GROUP_SEQS
    seq_ids = jnp.arange(GROUP_SEQS, dtype=jnp.int32)[None, :]
    lengths = jnp.where(seq_ids == longest, CACHE_MAX, lengths)
    lengths = jnp.where(seq_ids == shortest, 1, lengths)
    return by_group(lengths).astype(jnp.int32)


def draw_parents(key, part):
    node_ids = jnp.arange(TREE_ROWS, dtype=jnp.int32)
    ceiling = jnp.broadcast_to(jnp.maximum(node_ids, 1), (GROUPS, GROUP_SEQS, TREE_ROWS))
    picked = jax.random.randint(jax.random.fold_in(key, 7006), (GROUPS, GROUP_SEQS, TREE_ROWS), 0, ceiling, dtype=jnp.int32)
    picked = jnp.where(node_ids == 0, -1, picked)
    return by_group(picked).reshape(ATT_TP * GROUPS * GROUP_SEQS, TREE_ROWS).astype(jnp.int32)


def draw_w_out(key, part):
    base = jnp.clip(jax.random.normal(jax.random.fold_in(key, 7012), (ATT_TP, HEAD_SLICE, D_MODEL), jnp.float32), -6.0, 6.0) * 256.0 ** (-0.5)
    slice_ids = jnp.arange(ATT_TP * GROUPS, dtype=jnp.int32) // GROUPS
    return base[slice_ids].reshape(ATT_TP * GROUPS * HEAD_SLICE, D_MODEL).astype(jnp.bfloat16)


def route_block(single, favored):
    spread = MOST_ROWS - MEAN_LOAD
    ranked = jax.random.permutation(jax.random.fold_in(single, 1), EXPERTS).astype(jnp.int32)
    ranked = jnp.where(ranked == favored, ranked[0], ranked).at[0].set(favored)
    offsets = jax.random.randint(jax.random.fold_in(single, 2), (EXPERTS // 2,), 0, spread + 1, dtype=jnp.int32)
    offsets = offsets.at[0].set(spread)
    quotas = jnp.stack([MEAN_LOAD + offsets, MEAN_LOAD - offsets], axis=1).reshape(EXPERTS)
    boundary = jnp.cumsum(quotas)
    ticket = jnp.arange(ROWS_DEV * TOP_K, dtype=jnp.int32)
    position = jnp.sum((ticket[:, None] >= boundary[None, :]).astype(jnp.int32), axis=1)
    layout = ranked[position].reshape(TOP_K, ROWS_DEV).T
    row_order = jax.random.permutation(jax.random.fold_in(single, 3), ROWS_DEV)
    layout = layout[row_order]
    rotation = jax.random.randint(jax.random.fold_in(single, 4), (ROWS_DEV, 1), 0, TOP_K, dtype=jnp.int32)
    columns = (jnp.arange(TOP_K, dtype=jnp.int32)[None, :] + rotation) % TOP_K
    return jnp.take_along_axis(layout, columns, axis=1)


def draw_expert_ids(key, part):
    device_count = TOKENS // ROWS_DEV
    favored = jax.random.randint(jax.random.fold_in(key, 7007), (), 0, EXPERTS, dtype=jnp.int32)
    device_keys = jax.random.split(jax.random.fold_in(key, 7008), device_count)
    layouts = jax.vmap(lambda single: route_block(single, favored))(device_keys)
    return layouts.reshape(TOKENS, TOP_K).astype(jnp.int32)


def block_scale(stream_key, dims, pieces, low, high):
    def one(dim, parts):
        steps = jax.random.uniform(jax.random.fold_in(jax.random.fold_in(stream_key, 6), dim), (parts,), jnp.float32, low / len(pieces), high / len(pieces))
        return jnp.repeat(jnp.exp(steps), dims[dim] // parts).reshape((-1,) + (1,) * (len(dims) - dim - 1))

    loudness = one(*pieces[0])
    for cut in pieces[1:]:
        loudness = loudness * one(*cut)
    return loudness


def normal_values(rng, dims, deviation, most, cuts=(), held_as=jnp.bfloat16):
    factor_of = block_scale(rng, dims, cuts, -0.22, 0.18) if cuts else 1.0
    entries = jax.random.normal(rng, dims, jnp.float32) * deviation * factor_of
    return jnp.minimum(jnp.maximum(entries, -most), most).astype(held_as)


def setup_inputs(seed: int = 0, part: int = 0) -> dict:
    key_of = jax.random.split(jax.random.key(seed), 13)
    part_keys = jax.random.split(jax.random.fold_in(key_of[12], part), 13)
    queries = draw_queries(jax.random.fold_in(jax.random.fold_in(key_of[12], part), 71), part)
    tree_kv = draw_tree_kv(jax.random.fold_in(jax.random.fold_in(key_of[12], part), 71), part)
    kv_cache = draw_kv_cache(jax.random.fold_in(jax.random.fold_in(key_of[12], part), 71), part)
    block_table = draw_block_table(jax.random.fold_in(jax.random.fold_in(key_of[12], part), 71), part)
    cache_lengths = draw_cache_lengths(jax.random.fold_in(jax.random.fold_in(key_of[12], part), 71), part)
    parents = draw_parents(jax.random.fold_in(jax.random.fold_in(key_of[12], part), 71), part)
    w_out = draw_w_out(jax.random.fold_in(key_of[12], 71), part)
    w_gate = normal_values(key_of[7], (EXPERTS, D_MODEL, FF_EXP), D_MODEL ** -0.5, 0.125, ((0, 16),))
    w_up = normal_values(key_of[8], (EXPERTS, D_MODEL, FF_EXP), D_MODEL ** -0.5, 0.125, ((0, 16),))
    w_down = normal_values(key_of[9], (EXPERTS, FF_EXP, D_MODEL), 192 ** -0.5, 0.4375, ((0, 16),))
    expert_ids = draw_expert_ids(jax.random.fold_in(jax.random.fold_in(key_of[12], part), 71), part)
    gate_weights = jnp.clip(jnp.exp(math.log(0.5) - 2.3025851 * jax.random.uniform(part_keys[11], (TOKENS, TOP_K), jnp.float32) ** block_scale(part_keys[11], (TOKENS, TOP_K), ((0, 16),), -0.2, 0.2)), 0.05, 0.5)
    return dict(queries=queries, tree_kv=tree_kv, kv_cache=kv_cache, block_table=block_table, cache_lengths=cache_lengths, parents=parents, w_out=w_out, w_gate=w_gate, w_up=w_up, w_down=w_down, expert_ids=expert_ids, gate_weights=gate_weights)


def ancestor_mask(parents):
    node_ids = jnp.broadcast_to(jnp.arange(TREE_ROWS, dtype=jnp.int32), parents.shape)
    columns = jnp.arange(TREE_ROWS, dtype=jnp.int32)
    reached = node_ids[:, :, None] == columns
    for repeat in range(TREE_ROWS):
        safe_ids = jnp.maximum(node_ids, 0).astype(jnp.int32)
        parent_of = jnp.take_along_axis(parents, safe_ids, axis=1).astype(jnp.int32)
        node_ids = jnp.where(node_ids >= 0, parent_of, -1).astype(jnp.int32)
        reached = reached | (node_ids[:, :, None] == columns)
    return reached


def attend_sequences(query_rows, own_keys, own_values, cache_keys, cache_values, lengths, parents):
    seq_count = parents.shape[0]
    cached = cache_keys.shape[1]
    query_heads = query_rows.reshape(seq_count, TREE_ROWS, QH_DEV, HEAD_DIM).astype(jnp.float32)
    key_rows = jnp.concatenate([cache_keys, own_keys], axis=1).astype(jnp.float32)
    value_rows = jnp.concatenate([cache_values, own_values], axis=1).astype(jnp.float32)
    scores = jnp.einsum('sqhd,skd->sqhk', query_heads, key_rows, precision=lax.Precision.HIGHEST) * (HEAD_DIM ** -0.5)
    positions = jnp.arange(cached, dtype=jnp.int32)
    cache_open = jnp.broadcast_to(positions[None, None, :] < lengths[:, None, None], (seq_count, TREE_ROWS, cached))
    allowed = jnp.concatenate([cache_open, ancestor_mask(parents)], axis=2)[:, :, None, :]
    masked = jnp.where(allowed, scores, -jnp.inf)
    highest = jnp.max(masked, axis=-1, keepdims=True)
    weights = jnp.exp(masked - highest)
    denominator = jnp.sum(weights, axis=-1, keepdims=True)
    rounded = lax.optimization_barrier(weights.astype(jnp.bfloat16)).astype(jnp.float32)
    blended = jnp.einsum('sqhk,skd->sqhd', rounded, value_rows, precision=lax.Precision.HIGHEST)
    return (blended / denominator).reshape(seq_count * TREE_ROWS, QH_DEV * HEAD_DIM).astype(jnp.bfloat16)


def reference(queries, tree_kv, kv_cache, block_table, cache_lengths, parents, w_out, w_gate, w_up, w_down, expert_ids, gate_weights):
    key_pool = kv_cache[0]
    value_pool = kv_cache[1]

    def one_device(summed, device):
        first_row = (device * ROWS_G).astype(jnp.int32)
        first_seq = (device * GROUP_SEQS).astype(jnp.int32)
        query_rows = lax.dynamic_slice_in_dim(queries, first_row, ROWS_G, 0)
        own_keys = lax.dynamic_slice_in_dim(tree_kv[0], first_row, ROWS_G, 0).reshape(GROUP_SEQS, TREE_ROWS, HEAD_DIM)
        own_values = lax.dynamic_slice_in_dim(tree_kv[1], first_row, ROWS_G, 0).reshape(GROUP_SEQS, TREE_ROWS, HEAD_DIM)
        pages = (lax.dynamic_slice_in_dim(block_table, first_seq, GROUP_SEQS, 0) + device * POOL_DEV).astype(jnp.int32)
        cache_keys = key_pool[pages].reshape(GROUP_SEQS, CACHE_MAX, HEAD_DIM)
        cache_values = value_pool[pages].reshape(GROUP_SEQS, CACHE_MAX, HEAD_DIM)
        lengths = lax.dynamic_slice_in_dim(cache_lengths, device.astype(jnp.int32), 1, 0).reshape(GROUP_SEQS)
        local_parents = lax.dynamic_slice_in_dim(parents, first_seq, GROUP_SEQS, 0)
        slice_rows = lax.dynamic_slice_in_dim(w_out, (device * HEAD_SLICE).astype(jnp.int32), HEAD_SLICE, 0)
        attended = attend_sequences(query_rows, own_keys, own_values, cache_keys, cache_values, lengths, local_parents)
        projected = jnp.dot(attended, slice_rows, preferred_element_type=jnp.float32)
        group_slot = (device % GROUPS).astype(jnp.int32)
        return summed.at[group_slot].add(projected), None

    initial = jnp.zeros((GROUPS, ROWS_G, D_MODEL), jnp.float32)
    summed, unused = lax.scan(one_device, initial, jnp.arange(N_WIDE, dtype=jnp.int32))
    hidden = summed.astype(jnp.bfloat16).reshape(GROUPS, ATT_TP, ROWS_DEV, D_MODEL)
    hidden = jnp.transpose(hidden, (1, 0, 2, 3)).reshape(TOKENS, D_MODEL)

    capacity = N_WIDE * MOST_ROWS
    row_numbers = jnp.arange(TOKENS, dtype=jnp.int32)

    def expert_step(running, packed):
        number, gate_matrix, up_matrix, down_matrix = packed
        matches = expert_ids == number
        chosen = jnp.any(matches, axis=1)
        row_weight = jnp.sum(jnp.where(matches, gate_weights, 0.0), axis=1)
        ranking = jnp.cumsum(chosen.astype(jnp.int32)) - 1
        target = jnp.where(chosen, ranking, capacity).astype(jnp.int32)
        picked = jnp.zeros((capacity,), jnp.int32).at[target].set(row_numbers, mode='drop')
        occupied = jnp.zeros((capacity,), jnp.float32).at[target].set(1.0, mode='drop')
        inputs = hidden[picked]
        gate_part = jnp.dot(inputs, gate_matrix, preferred_element_type=jnp.float32)
        up_part = jnp.dot(inputs, up_matrix, preferred_element_type=jnp.float32)
        activated = (jax.nn.silu(gate_part) * up_part).astype(jnp.bfloat16)
        produced = jnp.dot(activated, down_matrix, preferred_element_type=jnp.float32).astype(jnp.bfloat16)
        scaled = produced.astype(jnp.float32) * (row_weight[picked] * occupied)[:, None]
        return running.at[picked].add(scaled), None

    initial_rows = jnp.zeros((TOKENS, D_MODEL), jnp.float32)
    combined, unused_rows = lax.scan(expert_step, initial_rows, (jnp.arange(EXPERTS, dtype=jnp.int32), w_gate, w_up, w_down))
    return combined.astype(jnp.bfloat16)
```

```python
import functools

import jax
import jax.numpy as jnp
from jax import lax
from jax.experimental import pallas as pl
from jax.experimental.pallas import tpu as pltpu
from jax.sharding import PartitionSpec as P

ATT_TP = 8
CHUNKS = 4
TILE = 256
LANES = 128
MESH = pl.DeviceIdType.MESH


def spread(bits):
    offsets = [0]
    for bit in bits:
        offsets += [offset + (1 << bit) for offset in offsets]
    return offsets


def swapped(bits, low):
    other = list(bits)
    if len(other) > low + 1:
        other[low], other[low + 1] = other[low + 1], other[low]
    return other


def layer_kernel(
    count,
    block_table,
    cache_lengths,
    queries_in,
    tree_in,
    cache_in,
    parents,
    w_out_in,
    w_gate_in,
    w_up_in,
    w_down_in,
    expert_ids,
    gate_weights,
    out,
    queries,
    tree,
    cache,
    w_out,
    w_gate,
    w_up,
    w_down,
    attended,
    partial,
    hidden,
    routing,
    gate_sum,
    up_sum,
    activated,
    produced,
    send_one,
    recv_one,
    send_two,
    recv_two,
    load_sem,
    one_send_sem,
    one_recv_sem,
    all_send_sem,
    all_recv_sem,
    route_send_sem,
    route_recv_sem,
    two_send_sem,
    two_recv_sem,
):
    me = lax.axis_index("wide")
    bit_count = count.bit_length() - 1
    slice_shift = bit_count - (ATT_TP.bit_length() - 1)
    mine = [(me // (1 << bit)) % 2 for bit in range(bit_count)]
    partner = [me + (1 - 2 * mine[bit]) * (1 << bit) for bit in range(bit_count)]

    barrier = pltpu.get_barrier_semaphore()
    for bit in range(bit_count):
        pl.semaphore_signal(
            barrier, inc=1, device_id={"wide": partner[bit]}, device_id_type=MESH
        )

    loads = []
    for number, (source, target) in enumerate(
        (
            (queries_in, queries),
            (tree_in, tree),
            (cache_in, cache),
            (w_out_in, w_out),
            (w_gate_in.at[0], w_gate),
            (w_up_in.at[0], w_up),
            (w_down_in.at[0], w_down),
        )
    ):
        copy = pltpu.make_async_copy(source, target, load_sem.at[number])
        copy.start()
        loads.append(copy)

    rows = out.shape[0]
    lane_ids = lax.broadcasted_iota(jnp.int32, (rows, routing.shape[2]), 1)
    row_weight = jnp.zeros((rows, routing.shape[2]), jnp.float32)
    for k in range(expert_ids.shape[1]):
        row_weight += jnp.where(
            expert_ids[:, k : k + 1] == lane_ids, gate_weights[:, k : k + 1], 0.0
        )
    routing[me] = row_weight

    seq_count, node_count = parents.shape
    head_dim = tree.shape[2]
    head_count = queries.shape[1] // head_dim
    page_count = block_table.shape[1]
    node_rows = lax.broadcasted_iota(jnp.int32, (node_count, node_count), 0)
    node_cols = lax.broadcasted_iota(jnp.int32, (node_count, node_count), 1)
    closures = []
    for seq in range(seq_count):
        linked = ((parents[seq : seq + 1, :] == node_rows) | (node_rows == node_cols)).astype(
            jnp.float32
        )
        closures.append(linked)
    for repeat in range(max(node_count - 1, 1).bit_length()):
        narrow = [linked.astype(jnp.bfloat16) for linked in closures]
        closures = [
            jnp.minimum(jnp.dot(linked, linked, preferred_element_type=jnp.float32), 1.0)
            for linked in narrow
        ]

    for copy in loads[:3]:
        copy.wait()
    cached = page_count * cache.shape[2]
    positions = lax.broadcasted_iota(jnp.int32, (head_count * node_count, cached), 1)
    across = (((1,), (1,)), ((), ()))
    for seq in range(seq_count):
        first = seq * node_count
        last = first + node_count
        stacked = jnp.concatenate(
            [
                queries[first:last, head * head_dim : (head + 1) * head_dim]
                for head in range(head_count)
            ],
            axis=0,
        )
        pages = [block_table[seq, page] for page in range(page_count)]
        keys = jnp.concatenate([cache[0, page] for page in pages], axis=0)
        values = jnp.concatenate([cache[1, page] for page in pages], axis=0)
        scale = head_dim ** (-0.5)
        cache_scores = (
            lax.dot_general(stacked, keys, across, preferred_element_type=jnp.float32) * scale
        )
        tree_scores = (
            lax.dot_general(
                stacked, tree[0, first:last], across, preferred_element_type=jnp.float32
            )
            * scale
        )
        seen = jnp.concatenate([closures[seq].T] * head_count, axis=0) > 0.5
        cache_scores = jnp.where(positions < cache_lengths[0, seq], cache_scores, -jnp.inf)
        tree_scores = jnp.where(seen, tree_scores, -jnp.inf)
        highest = jnp.maximum(
            jnp.max(cache_scores, axis=1, keepdims=True),
            jnp.max(tree_scores, axis=1, keepdims=True),
        )
        cache_probs = jnp.exp(cache_scores - highest)
        tree_probs = jnp.exp(tree_scores - highest)
        denominator = jnp.sum(cache_probs, axis=1, keepdims=True) + jnp.sum(
            tree_probs, axis=1, keepdims=True
        )
        blended = jnp.dot(
            cache_probs.astype(jnp.bfloat16), values, preferred_element_type=jnp.float32
        ) + jnp.dot(
            tree_probs.astype(jnp.bfloat16),
            tree[1, first:last],
            preferred_element_type=jnp.float32,
        )
        blended = (blended / denominator).astype(jnp.bfloat16)
        for head in range(head_count):
            attended[first:last, head * head_dim : (head + 1) * head_dim] = blended[
                head * node_count : (head + 1) * node_count
            ]

    started = []

    def send(source, target, send_sem, recv_sem, bit):
        copy = pltpu.make_async_remote_copy(
            src_ref=source,
            dst_ref=target,
            send_sem=send_sem,
            recv_sem=recv_sem,
            device_id={"wide": partner[bit]},
            device_id_type=MESH,
        )
        copy.start()
        started.append(copy)
        return copy

    width = w_out.shape[1] // CHUNKS
    spans = [slice(chunk * width, (chunk + 1) * width) for chunk in range(CHUNKS)]

    class Halving:
        def __init__(self, total, out_buffer, in_buffer, send_sems, recv_sems, shift, orders):
            self.total = total
            self.out_buffer = out_buffer
            self.in_buffer = in_buffer
            self.send_sems = send_sems
            self.recv_sems = recv_sems
            self.shift = shift
            self.orders = orders
            self.steps = len(orders[0])
            self.copies = {}

        def places(self, chunk, step):
            order = self.orders[chunk % 2]
            base = 0
            for bit in order[:step]:
                base = base + mine[bit] * (1 << (bit - self.shift))
            bit = order[step]
            offsets = spread([other - self.shift for other in order[step + 1 :]])
            weight = 1 << (bit - self.shift)
            kept = [base + mine[bit] * weight + offset for offset in offsets]
            sent = [base + (1 - mine[bit]) * weight + offset for offset in offsets]
            first = sum(1 << (self.steps - 1 - past) for past in range(step))
            return bit, kept, sent, first

        def start(self, chunk, step):
            bit, kept, sent, first = self.places(chunk, step)
            for number, place in enumerate(sent):
                self.out_buffer[chunk, first + number] = self.total[
                    place, :, spans[chunk]
                ].astype(jnp.bfloat16)
            region = pl.ds(first, len(sent))
            self.copies[chunk, step] = send(
                self.out_buffer.at[chunk, region],
                self.in_buffer.at[chunk, region],
                self.send_sems.at[chunk, step],
                self.recv_sems.at[chunk, step],
                bit,
            )

        def finish(self, chunk, step):
            bit, kept, sent, first = self.places(chunk, step)
            self.copies[chunk, step].wait_recv()
            for number, place in enumerate(kept):
                self.total[place, :, spans[chunk]] += self.in_buffer[
                    chunk, first + number
                ].astype(jnp.float32)

    class Doubling:
        def __init__(self, buffer, columns, send_sems, recv_sems, row, order):
            self.buffer = buffer
            self.columns = columns
            self.send_sems = send_sems
            self.recv_sems = recv_sems
            self.row = row
            self.order = order
            self.copies = {}

        def start(self, step):
            bit = self.order[step]
            offsets = [0]
            held = [me]
            for past in self.order[:step]:
                held += [place + (1 - 2 * mine[past]) * (1 << past) for place in held]
            for number, place in enumerate(held):
                view = self.buffer.at[place, :, self.columns]
                slot = (1 << step) - 1 + number
                self.copies[step, number] = send(
                    view, view, self.send_sems.at[self.row, slot],
                    self.recv_sems.at[self.row, slot], bit,
                )

        def finish(self, step):
            for number in range(1 << step):
                self.copies[step, number].wait_recv()

    all_bits = list(range(bit_count))
    slice_bits = all_bits[slice_shift:]
    first_sum = Halving(
        partial, send_one, recv_one, one_send_sem, one_recv_sem, slice_shift,
        (slice_bits, swapped(slice_bits, 0)),
    )
    second_orders = (all_bits, swapped(all_bits, 1))
    second_sum = Halving(
        produced, send_two, recv_two, two_send_sem, two_recv_sem, 0, second_orders
    )
    gathers = [
        Doubling(
            hidden, spans[chunk], all_send_sem, all_recv_sem, chunk, second_orders[chunk % 2][::-1]
        )
        for chunk in range(CHUNKS)
    ]
    route = Doubling(routing, slice(None), route_send_sem, route_recv_sem, 0, all_bits[::-1])

    loads[3].wait()
    pl.semaphore_wait(barrier, bit_count)
    for chunk in range(CHUNKS):
        projected = jnp.dot(
            attended[...], w_out[:, spans[chunk]], preferred_element_type=jnp.float32
        )
        partial[:, :, spans[chunk]] = projected.reshape(partial.shape[0], rows, width)
        first_sum.start(chunk, 0)
    route.start(0)
    for step in range(first_sum.steps):
        for chunk in range(CHUNKS):
            first_sum.finish(chunk, step)
            if step + 1 < first_sum.steps:
                first_sum.start(chunk, step + 1)
            else:
                hidden[me, :, spans[chunk]] = partial[
                    me // (1 << slice_shift), :, spans[chunk]
                ].astype(jnp.bfloat16)
                gathers[chunk].start(0)
    for step in range(bit_count):
        for chunk in range(CHUNKS):
            if step + 1 < bit_count:
                gathers[chunk].finish(step)
                gathers[chunk].start(step + 1)
        route.finish(step)
        if step + 1 < bit_count:
            route.start(step + 1)
    loads[4].wait()
    loads[5].wait()

    blocks = TILE // rows if count * rows > TILE else count
    groups = count // blocks
    tile_rows = blocks * rows
    hidden_width = w_gate.shape[1]
    cuts = [
        slice(start, min(start + TILE, hidden_width)) for start in range(0, hidden_width, TILE)
    ]

    def over_groups(step):
        if groups == 1:
            step(0)
        else:
            pl.loop(0, groups)(step)

    for chunk in range(CHUNKS):
        gathers[chunk].finish(bit_count - 1)

        def accumulate(group, chunk=chunk):
            taken = hidden[pl.ds(group * blocks, blocks), :, spans[chunk]].reshape(
                tile_rows, width
            )
            for cut in cuts:
                for sums, weights in ((gate_sum, w_gate), (up_sum, w_up)):
                    part = jnp.dot(
                        taken, weights[spans[chunk], cut], preferred_element_type=jnp.float32
                    )
                    if chunk == 0:
                        sums[group, :, cut] = part
                    else:
                        sums[group, :, cut] += part

        over_groups(accumulate)

    def activate(group):
        for cut in cuts:
            gate = gate_sum[group, :, cut]
            activated[group, :, cut] = (
                gate / (1.0 + jnp.exp(-gate)) * up_sum[group, :, cut]
            ).astype(jnp.bfloat16)

    over_groups(activate)
    loads[6].wait()
    for chunk in range(CHUNKS):

        def down(group, chunk=chunk):
            made = jnp.dot(
                activated[group], w_down[:, spans[chunk]], preferred_element_type=jnp.float32
            )
            table = routing[pl.ds(group * blocks, blocks)].reshape(tile_rows, routing.shape[2])
            experts = lax.broadcasted_iota(jnp.int32, table.shape, 1)
            weight = jnp.sum(jnp.where(experts == me, table, 0.0), axis=1, keepdims=True)
            produced[pl.ds(group * blocks, blocks), :, spans[chunk]] = (made * weight).reshape(
                blocks, rows, width
            )

        over_groups(down)
        second_sum.start(chunk, 0)
    for step in range(second_sum.steps):
        for chunk in range(CHUNKS):
            second_sum.finish(chunk, step)
            if step + 1 < second_sum.steps:
                second_sum.start(chunk, step + 1)
            else:
                out[:, spans[chunk]] = produced[me, :, spans[chunk]].astype(jnp.bfloat16)
    for copy in started:
        copy.wait_send()


def body(
    queries,
    tree_kv,
    kv_cache,
    block_table,
    cache_lengths,
    parents,
    w_out,
    w_gate,
    w_up,
    w_down,
    expert_ids,
    gate_weights,
):
    count = lax.axis_size("wide")
    rows = expert_ids.shape[0]
    features = w_out.shape[1]
    hidden_width = w_gate.shape[2]
    bit_count = count.bit_length() - 1
    slice_steps = ATT_TP.bit_length() - 1
    width = features // CHUNKS
    lanes = -(-count // LANES) * LANES
    blocks = TILE // rows if count * rows > TILE else count
    groups = count // blocks
    tile_rows = blocks * rows
    hbm = pl.BlockSpec(memory_space=pl.ANY)
    vmem = pl.BlockSpec(memory_space=pltpu.VMEM)
    smem = pl.BlockSpec(memory_space=pltpu.SMEM)
    dma = pltpu.SemaphoreType.DMA
    return pl.pallas_call(
        functools.partial(layer_kernel, count),
        out_shape=jax.ShapeDtypeStruct((rows, features), jnp.bfloat16),
        in_specs=[smem, smem, hbm, hbm, hbm, vmem, hbm, hbm, hbm, hbm, vmem, vmem],
        out_specs=vmem,
        scratch_shapes=[
            pltpu.VMEM(queries.shape, queries.dtype),
            pltpu.VMEM(tree_kv.shape, tree_kv.dtype),
            pltpu.VMEM(kv_cache.shape, kv_cache.dtype),
            pltpu.VMEM(w_out.shape, w_out.dtype),
            pltpu.VMEM(w_gate.shape[1:], w_gate.dtype),
            pltpu.VMEM(w_up.shape[1:], w_up.dtype),
            pltpu.VMEM(w_down.shape[1:], w_down.dtype),
            pltpu.VMEM(queries.shape, jnp.bfloat16),
            pltpu.VMEM((ATT_TP, rows, features), jnp.float32),
            pltpu.VMEM((count, rows, features), jnp.bfloat16),
            pltpu.VMEM((count, rows, lanes), jnp.float32),
            pltpu.VMEM((groups, tile_rows, hidden_width), jnp.float32),
            pltpu.VMEM((groups, tile_rows, hidden_width), jnp.float32),
            pltpu.VMEM((groups, tile_rows, hidden_width), jnp.bfloat16),
            pltpu.VMEM((count, rows, features), jnp.float32),
            pltpu.VMEM((CHUNKS, ATT_TP - 1, rows, width), jnp.bfloat16),
            pltpu.VMEM((CHUNKS, ATT_TP - 1, rows, width), jnp.bfloat16),
            pltpu.VMEM((CHUNKS, count - 1, rows, width), jnp.bfloat16),
            pltpu.VMEM((CHUNKS, count - 1, rows, width), jnp.bfloat16),
            dma((7,)),
            dma((CHUNKS, slice_steps)),
            dma((CHUNKS, slice_steps)),
            dma((CHUNKS, count - 1)),
            dma((CHUNKS, count - 1)),
            dma((1, count - 1)),
            dma((1, count - 1)),
            dma((CHUNKS, bit_count)),
            dma((CHUNKS, bit_count)),
        ],
        compiler_params=pltpu.CompilerParams(
            collective_id=0, has_side_effects=True, vmem_limit_bytes=60 << 20
        ),
    )(
        block_table,
        cache_lengths,
        queries,
        tree_kv,
        kv_cache,
        parents,
        w_out,
        w_gate,
        w_up,
        w_down,
        expert_ids,
        gate_weights,
    )


def solution(mesh):
    placed = (
        P(("groups", "wide"), None),
        P(None, ("groups", "wide"), None),
        P(None, ("groups", "wide"), None, None),
        P(("groups", "wide"), None),
        P(("groups", "wide"), None),
        P(("groups", "wide"), None),
        P("wide", None),
        P("wide", None, None),
        P("wide", None, None),
        P("wide", None, None),
        P(("groups", "wide"), None),
        P(("groups", "wide"), None),
    )
    return jax.shard_map(
        body, mesh=mesh, in_specs=placed, out_specs=P(("groups", "wide"), None), check_vma=False
    )
```

```python
import functools

import jax
import jax.numpy as jnp
from jax import lax
from jax.experimental import pallas as pl
from jax.experimental.pallas import tpu as pltpu
from jax.sharding import PartitionSpec as P

ATT_TP = 8
CHUNKS = 4
PERIOD = 2
TILE = 256
LANES = 128
MESH = pl.DeviceIdType.MESH


def spread(weights):
    offsets = [0]
    for weight in weights:
        offsets += [offset + weight for offset in offsets]
    return offsets


def swap_low(place):
    low, high = place // 2 % 2, place // 4 % 2
    return place - 2 * low - 4 * high + 4 * low + 2 * high


def swapped(bits, first, second):
    trade = {first: second, second: first}
    return [trade.get(bit, bit) for bit in bits]


def layer_kernel(
    count,
    block_table,
    cache_lengths,
    queries_in,
    tree_in,
    cache_in,
    parents,
    w_out_in,
    w_gate_in,
    w_up_in,
    w_down_in,
    expert_ids,
    gate_weights,
    out,
    queries,
    tree,
    cache,
    w_out,
    w_gate,
    w_up,
    w_down,
    attended,
    partial,
    hidden,
    routing,
    gate_sum,
    up_sum,
    activated,
    produced,
    send_one,
    recv_one,
    send_two,
    recv_two,
    load_sem,
    one_send_sem,
    one_recv_sem,
    all_send_sem,
    all_recv_sem,
    route_send_sem,
    route_recv_sem,
    two_send_sem,
    two_recv_sem,
):
    me = lax.axis_index("wide")
    bit_count = count.bit_length() - 1
    slice_shift = bit_count - (ATT_TP.bit_length() - 1)
    mine = [(me // (1 << bit)) % 2 for bit in range(bit_count)]
    partner = [me + (1 - 2 * mine[bit]) * (1 << bit) for bit in range(bit_count)]

    barrier = pltpu.get_barrier_semaphore()
    for bit in range(bit_count):
        pl.semaphore_signal(
            barrier, inc=1, device_id={"wide": partner[bit]}, device_id_type=MESH
        )

    loads = []
    for number, (source, target) in enumerate(
        (
            (queries_in, queries),
            (tree_in, tree),
            (cache_in, cache),
            (w_out_in, w_out),
            (w_gate_in.at[0], w_gate),
            (w_up_in.at[0], w_up),
            (w_down_in.at[0], w_down),
        )
    ):
        copy = pltpu.make_async_copy(source, target, load_sem.at[number])
        if number < 4:
            copy.start()
        loads.append(copy)

    rows = out.shape[0]
    ids = expert_ids[...].T
    weights_of = gate_weights[...].T
    lane_ids = lax.broadcasted_iota(jnp.int32, (rows, routing.shape[2]), 1)
    row_weight = jnp.zeros((rows, routing.shape[2]), jnp.float32)
    for k in range(expert_ids.shape[0]):
        row_weight += jnp.where(
            ids[:, k : k + 1] == lane_ids, weights_of[:, k : k + 1], 0.0
        )
    routing_rows = row_weight

    seq_count, node_count = parents.shape
    head_dim = tree.shape[2]
    head_count = queries.shape[1] // head_dim
    page_count = block_table.shape[1]
    node_rows = lax.broadcasted_iota(jnp.int32, (node_count, node_count), 0)
    node_cols = lax.broadcasted_iota(jnp.int32, (node_count, node_count), 1)
    closures = []
    for seq in range(seq_count):
        linked = ((parents[seq : seq + 1, :] == node_rows) | (node_rows == node_cols)).astype(
            jnp.float32
        )
        closures.append(linked)
    for repeat in range(max(node_count - 1, 1).bit_length()):
        narrow = [linked.astype(jnp.bfloat16) for linked in closures]
        closures = [
            jnp.minimum(jnp.dot(linked, linked, preferred_element_type=jnp.float32), 1.0)
            for linked in narrow
        ]

    for copy in loads[:3]:
        copy.wait()
    cached = page_count * cache.shape[2]
    positions = lax.broadcasted_iota(jnp.int32, (head_count * node_count, cached), 1)
    across = (((1,), (1,)), ((), ()))
    for seq in range(seq_count):
        first = seq * node_count
        last = first + node_count
        stacked = jnp.concatenate(
            [
                queries[first:last, head * head_dim : (head + 1) * head_dim]
                for head in range(head_count)
            ],
            axis=0,
        )
        pages = [block_table[seq, page] for page in range(page_count)]
        keys = jnp.concatenate([cache[0, page] for page in pages], axis=0)
        values = jnp.concatenate([cache[1, page] for page in pages], axis=0)
        scale = head_dim ** (-0.5)
        cache_scores = (
            lax.dot_general(stacked, keys, across, preferred_element_type=jnp.float32) * scale
        )
        tree_scores = (
            lax.dot_general(
                stacked, tree[0, first:last], across, preferred_element_type=jnp.float32
            )
            * scale
        )
        seen = jnp.concatenate([closures[seq].T] * head_count, axis=0) > 0.5
        cache_scores = jnp.where(positions < cache_lengths[0, seq], cache_scores, -jnp.inf)
        tree_scores = jnp.where(seen, tree_scores, -jnp.inf)
        highest = jnp.maximum(
            jnp.max(cache_scores, axis=1, keepdims=True),
            jnp.max(tree_scores, axis=1, keepdims=True),
        )
        cache_probs = jnp.exp(cache_scores - highest)
        tree_probs = jnp.exp(tree_scores - highest)
        denominator = jnp.sum(cache_probs, axis=1, keepdims=True) + jnp.sum(
            tree_probs, axis=1, keepdims=True
        )
        blended = jnp.dot(
            cache_probs.astype(jnp.bfloat16), values, preferred_element_type=jnp.float32
        ) + jnp.dot(
            tree_probs.astype(jnp.bfloat16),
            tree[1, first:last],
            preferred_element_type=jnp.float32,
        )
        blended = (blended / denominator).astype(jnp.bfloat16)
        for head in range(head_count):
            attended[first:last, head * head_dim : (head + 1) * head_dim] = blended[
                head * node_count : (head + 1) * node_count
            ]

    started = []

    def send(source, target, send_sem, recv_sem, bit):
        copy = pltpu.make_async_remote_copy(
            src_ref=source,
            dst_ref=target,
            send_sem=send_sem,
            recv_sem=recv_sem,
            device_id={"wide": partner[bit]},
            device_id_type=MESH,
        )
        copy.start()
        started.append(copy)
        return copy

    width = w_out.shape[1] // CHUNKS
    spans = [slice(chunk * width, (chunk + 1) * width) for chunk in range(CHUNKS)]

    class Halving:
        def __init__(self, total, out_buffer, in_buffer, send_sems, recv_sems, weights, orders):
            self.total = total
            self.out_buffer = out_buffer
            self.in_buffer = in_buffer
            self.send_sems = send_sems
            self.recv_sems = recv_sems
            self.weights = weights
            self.orders = orders
            self.steps = len(orders[0])
            self.copies = {}
            self.extra = []

        def places(self, chunk, step):
            order = self.orders[int(chunk % PERIOD == PERIOD - 1)]
            base = 0
            for bit in order[:step]:
                base = base + mine[bit] * self.weights[bit]
            bit = order[step]
            offsets = spread([self.weights[other] for other in order[step + 1 :]] + self.extra)
            weight = self.weights[bit]
            kept = [base + mine[bit] * weight + offset for offset in offsets]
            sent = [base + (1 - mine[bit]) * weight + offset for offset in offsets]
            first = sum(
                (1 << (self.steps - 1 - past)) << len(self.extra) for past in range(step)
            )
            return bit, kept, sent, first

        def start(self, chunk, step):
            self.fill(chunk, step)
            self.launch(chunk, step)

        def fill(self, chunk, step):
            bit, kept, sent, first = self.places(chunk, step)
            for number, place in enumerate(sent):
                self.out_buffer[chunk, first + number] = self.total[
                    place, :, spans[chunk]
                ].astype(jnp.bfloat16)

        def launch(self, chunk, step):
            bit, kept, sent, first = self.places(chunk, step)
            region = pl.ds(first, len(sent))
            self.copies[chunk, step] = send(
                self.out_buffer.at[chunk, region],
                self.in_buffer.at[chunk, region],
                self.send_sems.at[chunk, step],
                self.recv_sems.at[chunk, step],
                bit,
            )

        def finish(self, chunk, step):
            bit, kept, sent, first = self.places(chunk, step)
            self.copies[chunk, step].wait_recv()
            for number, place in enumerate(kept):
                self.total[place, :, spans[chunk]] += self.in_buffer[
                    chunk, first + number
                ].astype(jnp.float32)

    class Doubling:
        def __init__(self, buffer, send_sems, recv_sems, order):
            self.buffer = buffer
            self.send_sems = send_sems
            self.recv_sems = recv_sems
            self.order = order
            self.copies = {}

        def base(self, step):
            place = 0
            for later in range(step, bit_count):
                place = place + mine[self.order[later]] * (1 << later)
            return place

        def start(self, step):
            view = self.buffer.at[pl.ds(self.base(step), 1 << step)]
            self.copies[step] = send(
                view, view, self.send_sems.at[step], self.recv_sems.at[step], self.order[step]
            )

        def finish(self, step):
            self.copies[step].wait_recv()

    all_bits = list(range(bit_count))
    slice_bits = all_bits[slice_shift:]
    trade = (bit_count - 2, bit_count - 3)
    far_bit = slice_bits[-1]
    slice_weights = {bit: 1 << (bit - slice_shift) for bit in slice_bits}
    place_weights = {bit: 1 << (bit_count - 1 - bit) for bit in all_bits}
    first_sum = Halving(
        partial, send_one, recv_one, one_send_sem, one_recv_sem, slice_weights,
        (slice_bits[:-1], swapped(slice_bits[:-1], *trade)),
    )
    first_sum.extra = [slice_weights[far_bit]]
    second_orders = (all_bits, swapped(all_bits, *trade))
    second_sum = Halving(
        produced, send_two, recv_two, two_send_sem, two_recv_sem, place_weights, second_orders
    )
    gathers = [
        Doubling(
            hidden.at[chunk], all_send_sem.at[chunk], all_recv_sem.at[chunk],
            second_orders[int(chunk % PERIOD == PERIOD - 1)][::-1],
        )
        for chunk in range(CHUNKS)
    ]
    route = Doubling(routing, route_send_sem, route_recv_sem, all_bits[::-1])
    my_place = route.base(0)
    routing[my_place] = routing_rows

    last_step = len(slice_bits) - 1
    far_first = (1 << last_step) * 2 - 2

    def far_places():
        base = 0
        for bit in slice_bits[:-1]:
            base = base + mine[bit] * slice_weights[bit]
        return [base, base + slice_weights[far_bit]]

    far_copies = {}

    def far_start(chunk):
        for number, place in enumerate(far_places()):
            send_one[chunk, far_first + number] = partial[place, :, spans[chunk]].astype(
                jnp.bfloat16
            )
        region = pl.ds(far_first, 2)
        far_copies[chunk] = send(
            send_one.at[chunk, region], recv_one.at[chunk, region],
            one_send_sem.at[chunk, last_step], one_recv_sem.at[chunk, last_step], far_bit,
        )

    def far_finish(chunk):
        far_copies[chunk].wait_recv()
        base = gathers[chunk].base(1)
        for number, place in enumerate(far_places()):
            hidden[chunk, base + number] = (
                partial[place, :, spans[chunk]]
                + recv_one[chunk, far_first + number].astype(jnp.float32)
            ).astype(jnp.bfloat16)

    loads[3].wait()
    for copy in loads[4:]:
        copy.start()
    for chunk in range(CHUNKS):
        projected = jnp.dot(
            attended[...], w_out[:, spans[chunk]], preferred_element_type=jnp.float32
        )
        partial[:, :, spans[chunk]] = projected.reshape(partial.shape[0], rows, width)
        first_sum.fill(chunk, 0)
    pl.semaphore_wait(barrier, bit_count)
    for chunk in range(CHUNKS):
        first_sum.launch(chunk, 0)
    route.start(0)
    for step in range(last_step):
        for chunk in range(CHUNKS):
            first_sum.finish(chunk, step)
            if step + 1 < last_step:
                first_sum.start(chunk, step + 1)
            else:
                far_start(chunk)
    route.finish(0)
    route.start(1)
    for chunk in range(CHUNKS):
        far_finish(chunk)
        gathers[chunk].start(1)
    for step in range(1, bit_count):
        for chunk in range(CHUNKS):
            if step + 1 < bit_count:
                gathers[chunk].finish(step)
                gathers[chunk].start(step + 1)
        route.finish(step)
        if step + 1 < bit_count:
            route.start(step + 1)
    loads[4].wait()
    loads[5].wait()

    blocks = TILE // rows if count * rows > TILE else count
    groups = count // blocks
    tile_rows = blocks * rows
    hidden_width = w_gate.shape[1]
    cuts = [
        slice(start, min(start + TILE, hidden_width)) for start in range(0, hidden_width, TILE)
    ]

    def over_groups(step):
        if groups == 1:
            step(0)
        else:
            pl.loop(0, groups)(step)

    for chunk in range(CHUNKS):
        gathers[chunk].finish(bit_count - 1)

        def accumulate(group, chunk=chunk):
            taken = hidden[chunk, pl.ds(group * blocks, blocks)]
            if chunk % PERIOD == PERIOD - 1:
                order = [swap_low(block) for block in range(blocks)]
                taken = jnp.concatenate([taken[block : block + 1] for block in order], axis=0)
            taken = taken.reshape(tile_rows, width)
            for cut in cuts:
                for sums, weights in ((gate_sum, w_gate), (up_sum, w_up)):
                    part = jnp.dot(
                        taken, weights[spans[chunk], cut], preferred_element_type=jnp.float32
                    )
                    if chunk == 0:
                        sums[group, :, cut] = part
                    else:
                        sums[group, :, cut] += part

        over_groups(accumulate)

    def activate(group):
        for cut in cuts:
            gate = gate_sum[group, :, cut]
            activated[group, :, cut] = (
                gate / (1.0 + jnp.exp(-gate)) * up_sum[group, :, cut]
            ).astype(jnp.bfloat16)

    over_groups(activate)
    loads[6].wait()
    for chunk in range(CHUNKS):

        def down(group, chunk=chunk):
            made = jnp.dot(
                activated[group], w_down[:, spans[chunk]], preferred_element_type=jnp.float32
            )
            table = routing[pl.ds(group * blocks, blocks)].reshape(tile_rows, routing.shape[2])
            experts = lax.broadcasted_iota(jnp.int32, table.shape, 1)
            weight = jnp.sum(jnp.where(experts == me, table, 0.0), axis=1, keepdims=True)
            produced[pl.ds(group * blocks, blocks), :, spans[chunk]] = (made * weight).reshape(
                blocks, rows, width
            )

        over_groups(down)
        second_sum.start(chunk, 0)
    for step in range(second_sum.steps):
        for chunk in range(CHUNKS):
            second_sum.finish(chunk, step)
            if step + 1 < second_sum.steps:
                second_sum.start(chunk, step + 1)
            else:
                out[:, spans[chunk]] = produced[my_place, :, spans[chunk]].astype(jnp.bfloat16)
    for copy in started:
        copy.wait_send()


def body(
    queries,
    tree_kv,
    kv_cache,
    block_table,
    cache_lengths,
    parents,
    w_out,
    w_gate,
    w_up,
    w_down,
    expert_ids,
    gate_weights,
):
    count = lax.axis_size("wide")
    rows = expert_ids.shape[0]
    features = w_out.shape[1]
    hidden_width = w_gate.shape[2]
    bit_count = count.bit_length() - 1
    slice_steps = ATT_TP.bit_length() - 1
    width = features // CHUNKS
    lanes = -(-count // LANES) * LANES
    blocks = TILE // rows if count * rows > TILE else count
    groups = count // blocks
    tile_rows = blocks * rows
    hbm = pl.BlockSpec(memory_space=pl.ANY)
    vmem = pl.BlockSpec(memory_space=pltpu.VMEM)
    smem = pl.BlockSpec(memory_space=pltpu.SMEM)
    dma = pltpu.SemaphoreType.DMA
    return pl.pallas_call(
        functools.partial(layer_kernel, count),
        out_shape=jax.ShapeDtypeStruct((rows, features), jnp.bfloat16),
        in_specs=[smem, smem, hbm, hbm, hbm, vmem, hbm, hbm, hbm, hbm, vmem, vmem],
        out_specs=vmem,
        scratch_shapes=[
            pltpu.VMEM(queries.shape, queries.dtype),
            pltpu.VMEM(tree_kv.shape, tree_kv.dtype),
            pltpu.VMEM(kv_cache.shape, kv_cache.dtype),
            pltpu.VMEM(w_out.shape, w_out.dtype),
            pltpu.VMEM(w_gate.shape[1:], w_gate.dtype),
            pltpu.VMEM(w_up.shape[1:], w_up.dtype),
            pltpu.VMEM(w_down.shape[1:], w_down.dtype),
            pltpu.VMEM(queries.shape, jnp.bfloat16),
            pltpu.VMEM((ATT_TP, rows, features), jnp.float32),
            pltpu.VMEM((CHUNKS, count, rows, width), jnp.bfloat16),
            pltpu.VMEM((count, rows, lanes), jnp.float32),
            pltpu.VMEM((groups, tile_rows, hidden_width), jnp.float32),
            pltpu.VMEM((groups, tile_rows, hidden_width), jnp.float32),
            pltpu.VMEM((groups, tile_rows, hidden_width), jnp.bfloat16),
            pltpu.VMEM((count, rows, features), jnp.float32),
            pltpu.VMEM((CHUNKS, ATT_TP, rows, width), jnp.bfloat16),
            pltpu.VMEM((CHUNKS, ATT_TP, rows, width), jnp.bfloat16),
            pltpu.VMEM((CHUNKS, count - 1, rows, width), jnp.bfloat16),
            pltpu.VMEM((CHUNKS, count - 1, rows, width), jnp.bfloat16),
            dma((7,)),
            dma((CHUNKS, slice_steps)),
            dma((CHUNKS, slice_steps)),
            dma((CHUNKS, bit_count)),
            dma((CHUNKS, bit_count)),
            dma((bit_count,)),
            dma((bit_count,)),
            dma((CHUNKS, bit_count)),
            dma((CHUNKS, bit_count)),
        ],
        compiler_params=pltpu.CompilerParams(
            collective_id=0, has_side_effects=True, vmem_limit_bytes=60 << 20
        ),
    )(
        block_table,
        cache_lengths,
        queries,
        tree_kv,
        kv_cache,
        parents,
        w_out,
        w_gate,
        w_up,
        w_down,
        expert_ids.T,
        gate_weights.T,
    )


def solution(mesh):
    placed = (
        P(("groups", "wide"), None),
        P(None, ("groups", "wide"), None),
        P(None, ("groups", "wide"), None, None),
        P(("groups", "wide"), None),
        P(("groups", "wide"), None),
        P(("groups", "wide"), None),
        P("wide", None),
        P("wide", None, None),
        P("wide", None, None),
        P("wide", None, None),
        P(("groups", "wide"), None),
        P(("groups", "wide"), None),
    )
    return jax.shard_map(
        body, mesh=mesh, in_specs=placed, out_specs=P(("groups", "wide"), None), check_vma=False
    )
```
